256 devices in a mesh: seq: 16 (over y, x), dp: 16 (over z, core).
Axes of the slice: x: 4, y: 4, z: 8, core: 2. Of those that a mesh axis runs over, the one named last changes fastest.
Arguments:
- queries: bfloat16 [128, 256, 4096], P(None, ('seq', 'dp')), may hold values from -8 to 8
- keys_in: bfloat16 [128, 256, 4096], P(None, ('seq', 'dp')), may hold values from -8 to 8
- values: bfloat16 [128, 256, 4096], P(None, ('seq', 'dp')), may hold values from -6 to 6
- grad_out: bfloat16 [10, 4096, 4096], P(None, ('seq', 'dp')), may hold values from -6 to 6
- doc_lengths: int32 [24], replicated, may hold values from 1 to 2560, as said below
- doc_group: int32 [24], replicated, may hold values from 0 to 15, as said below
Outputs:
- attended: bfloat16 [10, 4096, 4096], P(None, ('seq', 'dp'))
- grad_queries: bfloat16 [128, 256, 4096], P(None, ('seq', 'dp'))
- grad_keys: bfloat16 [128, 256, 4096], P(None, ('seq', 'dp'))
- grad_values: bfloat16 [128, 256, 4096], P(None, ('seq', 'dp'))
The draws below stay inside these ranges and needn't reach their ends.
Inputs may be any that keep to these rules, and one draw needn't show every extreme that they name: `doc_lengths`: the documents lie one after another in the packed batch in index order and their lengths sum to 32768. The documents of one group are consecutive, groups in increasing order; every group holds a whole multiple of 256 tokens, at most 2560, and some group holds exactly that many. `doc_group`: never falls from one document to the next; every group takes at least one document.
All inputs are finite; a program needn't handle non-finite values.
Results may differ from the reference program's by a relative error of at most 0.02.
Values may be sent and summed in bfloat16 or wider, within the bound.
A program may use at most 64 MiB of HBM per device.

```python
import jax
import jax.numpy as jnp
from jax import lax

HEADS = 32
HEAD = 128
TOK_DEV = 128
MAXLEN = 4096
FEAT = 4096
CAP = 10
NDOC = 24
N_SEQ = 16
N_DP = 16


def packing_layout(key):
    devices = N_SEQ * N_DP
    base_key = jax.random.fold_in(key, 7001)
    big_key = jax.random.fold_in(base_key, 1)
    unit_key = jax.random.fold_in(base_key, 2)
    extra_key = jax.random.fold_in(base_key, 3)
    length_key = jax.random.fold_in(base_key, 4)
    largest = jax.random.randint(big_key, (), 0, N_DP).astype(jnp.int32)
    group_ids = jnp.arange(N_DP, dtype=jnp.int32)
    group_units = jnp.where(group_ids == largest, CAP, 1).astype(jnp.int32)

    def add_unit(number, counts):
        scores = jax.random.randint(jax.random.fold_in(unit_key, number), (N_DP,), 0, 1 << 20).astype(jnp.int32) * N_DP + group_ids
        scores = jnp.where((counts < CAP) & (group_ids != largest), scores, -1)
        chosen = jnp.argmax(scores).astype(jnp.int32)
        return counts.at[chosen].add(1)
    group_units = lax.fori_loop(0, TOK_DEV - CAP - (N_DP - 1), add_unit, group_units)
    group_tokens = (group_units * devices).astype(jnp.int32)
    doc_counts = ((group_tokens + MAXLEN - 1) // MAXLEN).astype(jnp.int32)
    spare_docs = NDOC - jnp.sum(doc_counts)

    def add_doc(number, counts):
        drawn_group = jax.random.randint(jax.random.fold_in(extra_key, number), (), 0, N_DP - 1).astype(jnp.int32)
        chosen = jnp.where(drawn_group >= largest, drawn_group + 1, drawn_group)
        return jnp.where(number < spare_docs, counts.at[chosen].add(1), counts)
    doc_counts = lax.fori_loop(0, NDOC, add_doc, doc_counts)
    doc_ids = jnp.arange(NDOC, dtype=jnp.int32)
    doc_ends = jnp.cumsum(doc_counts).astype(jnp.int32)
    doc_group = jnp.sum(doc_ends[None, :] <= doc_ids[:, None], axis=1).astype(jnp.int32)
    first_doc = (doc_ends - doc_counts).astype(jnp.int32)
    forced = min(MAXLEN, CAP * devices)

    def place(number, loop_state):
        left_tokens, left_docs, lengths = loop_state
        owner_group = doc_group[number]
        remain = left_tokens[owner_group]
        docs_left = left_docs[owner_group]
        lowest = jnp.maximum(1, remain - (docs_left - 1) * MAXLEN)
        highest = jnp.minimum(MAXLEN, remain - (docs_left - 1))
        chosen = jax.random.randint(jax.random.fold_in(length_key, number), (), lowest, highest + 1).astype(jnp.int32)
        chosen = jnp.where((owner_group == largest) & (number == first_doc[owner_group]), forced, chosen).astype(jnp.int32)
        return (left_tokens.at[owner_group].add(-chosen), left_docs.at[owner_group].add(-1), lengths.at[number].set(chosen))
    loop_state = lax.fori_loop(0, NDOC, place, (group_tokens, doc_counts, jnp.zeros((NDOC,), jnp.int32)))
    return (loop_state[2], doc_group)


def draw_doc_lengths(key, part):
    return packing_layout(key)[0]


def draw_doc_group(key, part):
    return packing_layout(key)[1]


def attention_rows(key, which_one):
    devices = N_SEQ * N_DP
    tokens = TOK_DEV * devices
    features = HEADS * HEAD
    own_key = jax.random.fold_in(key, 9100 + which_one)
    drawn_rows = jnp.clip(1.6 * jax.random.normal(own_key, (tokens, features), jnp.float32), -8.0, 8.0)
    return drawn_rows.reshape(TOK_DEV, devices, features).astype(jnp.bfloat16)


def draw_queries(key, part):
    return attention_rows(key, 0)


def draw_keys_in(key, part):
    return attention_rows(key, 1)


def levels(key, extent, shards, least, top_value):
    def one(position, parts):
        steps = jax.random.uniform(jax.random.fold_in(jax.random.fold_in(key, 6), position), (parts,), jnp.float32, least / len(shards), top_value / len(shards))
        return jnp.repeat(jnp.exp(steps), extent[position] // parts).reshape((-1,) + (1,) * (len(extent) - position - 1))

    level = one(*shards[0])
    for cut in shards[1:]:
        level = level * one(*cut)
    return level


def scatter_about(key, extent, width, limit, pieces=(), held_as=jnp.bfloat16):
    array = width * jax.random.normal(key, extent, jnp.float32)
    if pieces:
        array = array * levels(key, extent, pieces, -0.22, 0.18)
    return jnp.clip(array, -limit, limit).astype(held_as)


def setup_inputs(seed: int = 0) -> dict:
    key_of = jax.random.split(jax.random.key(seed), 7)
    return {
        "queries": draw_queries(jax.random.fold_in(key_of[6], 71), 0),
        "keys_in": draw_keys_in(jax.random.fold_in(key_of[6], 71), 0),
        "values": scatter_about(key_of[2], (TOK_DEV, N_SEQ * N_DP, FEAT), 1.0, 6.0, ((1, 256),)),
        "grad_out": scatter_about(key_of[3], (CAP, N_SEQ * N_DP * N_DP, FEAT), 1.0, 6.0, ((1, 256),)),
        "doc_lengths": draw_doc_lengths(jax.random.fold_in(key_of[6], 71), 0),
        "doc_group": draw_doc_group(jax.random.fold_in(key_of[6], 71), 0),
    }


NEGATIVE_FILL = -1.0e30


def layout_tables(doc_lengths, doc_group):
    devices = N_SEQ * N_DP
    doc_ends = jnp.cumsum(doc_lengths).astype(jnp.int32)
    member = (doc_group[:, None] == jnp.arange(N_DP, dtype=jnp.int32)[None, :]).astype(jnp.int32)
    group_units = (jnp.sum(member * doc_lengths[:, None], axis=0) // devices).astype(jnp.int32)
    first_unit = (jnp.cumsum(group_units) - group_units).astype(jnp.int32)
    return doc_ends, group_units, first_unit


def reference(queries, keys_in, values, grad_out, doc_lengths, doc_group):
    devices = N_SEQ * N_DP
    tokens = TOK_DEV * devices
    features = HEADS * HEAD
    key_span = min(MAXLEN, CAP * devices)
    block_rows = min(512, tokens)
    blocks = tokens // block_rows
    window = block_rows + key_span
    score_scale = HEAD ** -0.5
    doc_ends, group_units, first_unit = layout_tables(doc_lengths, doc_group)
    positions = jnp.arange(tokens, dtype=jnp.int32)
    doc_of = jnp.sum(doc_ends[None, :] <= positions[:, None], axis=1).astype(jnp.int32)
    unit_of = (positions // devices).astype(jnp.int32)
    device_of = (positions % devices).astype(jnp.int32)
    group_of = jnp.sum((first_unit + group_units)[None, :] <= unit_of[:, None], axis=1).astype(jnp.int32)
    slot_of = (unit_of - jnp.take(first_unit, group_of)).astype(jnp.int32)
    column_of = (((device_of // N_DP) * N_DP + group_of) * N_DP + device_of % N_DP).astype(jnp.int32)
    balanced_of = (slot_of * (devices * N_DP) + column_of).astype(jnp.int32)

    head_shape = (tokens, HEADS, HEAD)
    query_all = queries.reshape(head_shape)
    key_all = keys_in.reshape(head_shape)
    value_all = values.reshape(head_shape)
    cot_all = jnp.take(grad_out.reshape(CAP * devices * N_DP, features), balanced_of, axis=0).reshape(head_shape)

    front_pad = jnp.zeros((key_span, HEADS, HEAD), keys_in.dtype)
    key_front = jnp.concatenate([front_pad, key_all], axis=0)
    value_front = jnp.concatenate([front_pad, value_all], axis=0)
    docs_front = jnp.concatenate([jnp.full((key_span,), -1, jnp.int32), doc_of])
    pos_front = jnp.concatenate([jnp.zeros((key_span,), jnp.int32), positions])

    def masked_scores(q_rows, k_rows, q_docs, k_docs, q_pos, k_pos):
        scores = jnp.einsum('qhe,khe->qhk', q_rows.astype(jnp.float32), k_rows.astype(jnp.float32)) * score_scale
        allowed = (q_docs[:, None] == k_docs[None, :]) & (k_pos[None, :] <= q_pos[:, None])
        return scores, allowed[:, None, :]

    def forward_block(number):
        start = number * block_rows
        q_rows = lax.dynamic_slice_in_dim(query_all, start, block_rows, 0)
        k_rows = lax.dynamic_slice_in_dim(key_front, start, window, 0)
        v_rows = lax.dynamic_slice_in_dim(value_front, start, window, 0)
        scores, allowed = masked_scores(q_rows, k_rows,
                                        lax.dynamic_slice_in_dim(doc_of, start, block_rows, 0),
                                        lax.dynamic_slice_in_dim(docs_front, start, window, 0),
                                        lax.dynamic_slice_in_dim(positions, start, block_rows, 0),
                                        lax.dynamic_slice_in_dim(pos_front, start, window, 0))
        row_top = jnp.max(jnp.where(allowed, scores, NEGATIVE_FILL), axis=2, keepdims=True)
        row_total = jnp.sum(jnp.where(allowed, jnp.exp(scores - row_top), 0.0), axis=2, keepdims=True)
        log_total = row_top + jnp.log(row_total)
        weight = jnp.where(allowed, jnp.exp(scores - log_total), 0.0).astype(jnp.bfloat16)
        block_out = jnp.einsum('qhk,khe->qhe', weight.astype(jnp.float32), v_rows.astype(jnp.float32)).astype(jnp.bfloat16)
        return block_out, log_total[:, :, 0]

    out_blocks, log_blocks = lax.map(forward_block, jnp.arange(blocks, dtype=jnp.int32))
    out_all = out_blocks.reshape(head_shape)
    log_all = log_blocks.reshape(tokens, HEADS)
    delta_all = jnp.sum(cot_all.astype(jnp.float32) * out_all.astype(jnp.float32), axis=2)

    def query_grad_block(number):
        start = number * block_rows
        q_rows = lax.dynamic_slice_in_dim(query_all, start, block_rows, 0)
        k_rows = lax.dynamic_slice_in_dim(key_front, start, window, 0)
        v_rows = lax.dynamic_slice_in_dim(value_front, start, window, 0)
        cot_rows = lax.dynamic_slice_in_dim(cot_all, start, block_rows, 0)
        scores, allowed = masked_scores(q_rows, k_rows,
                                        lax.dynamic_slice_in_dim(doc_of, start, block_rows, 0),
                                        lax.dynamic_slice_in_dim(docs_front, start, window, 0),
                                        lax.dynamic_slice_in_dim(positions, start, block_rows, 0),
                                        lax.dynamic_slice_in_dim(pos_front, start, window, 0))
        row_log = lax.dynamic_slice_in_dim(log_all, start, block_rows, 0)
        row_delta = lax.dynamic_slice_in_dim(delta_all, start, block_rows, 0)
        weight_full = jnp.where(allowed, jnp.exp(scores - row_log[:, :, None]), 0.0)
        grad_prob = jnp.einsum('qhe,khe->qhk', cot_rows.astype(jnp.float32), v_rows.astype(jnp.float32))
        grad_score = (weight_full * (grad_prob - row_delta[:, :, None])).astype(jnp.bfloat16)
        return (jnp.einsum('qhk,khe->qhe', grad_score.astype(jnp.float32), k_rows.astype(jnp.float32)) * score_scale).astype(jnp.bfloat16)

    grad_q_all = lax.map(query_grad_block, jnp.arange(blocks, dtype=jnp.int32)).reshape(head_shape)

    back_pad = jnp.zeros((key_span, HEADS, HEAD), queries.dtype)
    query_back = jnp.concatenate([query_all, back_pad], axis=0)
    cot_back = jnp.concatenate([cot_all, back_pad.astype(cot_all.dtype)], axis=0)
    docs_back = jnp.concatenate([doc_of, jnp.full((key_span,), -2, jnp.int32)])
    pos_back = jnp.concatenate([positions, jnp.zeros((key_span,), jnp.int32)])
    log_back = jnp.concatenate([log_all, jnp.zeros((key_span, HEADS), log_all.dtype)], axis=0)
    delta_back = jnp.concatenate([delta_all, jnp.zeros((key_span, HEADS), delta_all.dtype)], axis=0)

    def key_grad_block(number):
        start = number * block_rows
        k_rows = lax.dynamic_slice_in_dim(key_all, start, block_rows, 0)
        v_rows = lax.dynamic_slice_in_dim(value_all, start, block_rows, 0)
        q_rows = lax.dynamic_slice_in_dim(query_back, start, window, 0)
        cot_rows = lax.dynamic_slice_in_dim(cot_back, start, window, 0)
        scores, allowed = masked_scores(q_rows, k_rows,
                                        lax.dynamic_slice_in_dim(docs_back, start, window, 0),
                                        lax.dynamic_slice_in_dim(doc_of, start, block_rows, 0),
                                        lax.dynamic_slice_in_dim(pos_back, start, window, 0),
                                        lax.dynamic_slice_in_dim(positions, start, block_rows, 0))
        row_log = lax.dynamic_slice_in_dim(log_back, start, window, 0)
        row_delta = lax.dynamic_slice_in_dim(delta_back, start, window, 0)
        weight_full = jnp.where(allowed, jnp.exp(scores - row_log[:, :, None]), 0.0)
        weight = weight_full.astype(jnp.bfloat16)
        grad_v = jnp.einsum('qhk,qhe->khe', weight.astype(jnp.float32), cot_rows.astype(jnp.float32)).astype(jnp.bfloat16)
        grad_prob = jnp.einsum('qhe,khe->qhk', cot_rows.astype(jnp.float32), v_rows.astype(jnp.float32))
        grad_score = (weight_full * (grad_prob - row_delta[:, :, None])).astype(jnp.bfloat16)
        grad_k = (jnp.einsum('qhk,qhe->khe', grad_score.astype(jnp.float32), q_rows.astype(jnp.float32)) * score_scale).astype(jnp.bfloat16)
        return grad_k, grad_v

    grad_k_blocks, grad_v_blocks = lax.map(key_grad_block, jnp.arange(blocks, dtype=jnp.int32))

    slot_ids = jnp.arange(CAP * devices * N_DP, dtype=jnp.int32)
    slot_c = (slot_ids // (devices * N_DP)).astype(jnp.int32)
    column = (slot_ids % (devices * N_DP)).astype(jnp.int32)
    group_c = ((column // N_DP) % N_DP).astype(jnp.int32)
    seq_c = (column // (N_DP * N_DP)).astype(jnp.int32)
    data_c = (column % N_DP).astype(jnp.int32)
    slot_live = slot_c < jnp.take(group_units, group_c)
    source = (jnp.take(first_unit, group_c) + slot_c) * devices + seq_c * N_DP + data_c
    source = jnp.where(slot_live, source, 0).astype(jnp.int32)
    out_flat = out_all.reshape(tokens, features)
    attended = jnp.where(slot_live[:, None], jnp.take(out_flat, source, axis=0), jnp.zeros((), out_flat.dtype))
    attended = attended.reshape(CAP, devices * N_DP, features)

    packed_shape = (TOK_DEV, devices, features)
    return (attended, grad_q_all.reshape(packed_shape), grad_k_blocks.reshape(packed_shape), grad_v_blocks.reshape(packed_shape))
```

```python
import functools

import jax
import jax.numpy as jnp
import numpy as np
from jax import lax
from jax.experimental import pallas as pl
from jax.experimental.pallas import tpu as pltpu
from jax.sharding import PartitionSpec as P

HEAD = 128
NEGATIVE_FILL = -1e30
LOG2E = 1.4426950408889634
BLOCK = 512
MESH = pl.DeviceIdType.MESH


def group_tables(doc_lengths, doc_group, group_count, per_unit):
    doc_ends = jnp.cumsum(doc_lengths)
    member = (doc_group[:, None] == jnp.arange(group_count, dtype=jnp.int32)[None, :]).astype(
        jnp.int32
    )
    group_units = jnp.sum(member * doc_lengths[:, None], axis=0) // per_unit
    first_unit = jnp.cumsum(group_units) - group_units
    return (doc_ends, group_units, first_unit)


def greet_all(seq, dp, n_seq, n_dp):
    me = seq * n_dp + dp
    total = n_seq * n_dp
    barrier = pltpu.get_barrier_semaphore()

    def greet(offset, carry):
        peer = lax.rem(me + offset, total)
        pl.semaphore_signal(
            barrier, 1, device_id=(peer // n_dp, lax.rem(peer, n_dp)), device_id_type=MESH
        )
        return carry

    lax.fori_loop(1, total, greet, 0)
    pl.semaphore_wait(barrier, total - 1)


def scatter_kernel(n_seq, n_dp, packed, cot, out, send_sem, recv_sem, cot_send, cot_recv):
    seq, dp = lax.axis_index("seq"), lax.axis_index("dp")
    total = n_seq * n_dp
    me = seq * n_dp + dp
    greet_all(seq, dp, n_seq, n_dp)

    def send_cot(offset, carry):
        peer = lax.rem(seq + offset, n_seq)
        pltpu.make_async_remote_copy(
            cot.at[:, :, peer],
            out.at[3, :, pl.ds(seq * n_dp, n_dp)],
            cot_send,
            cot_recv,
            device_id=(peer, dp),
            device_id_type=MESH,
        ).start()
        return carry

    lax.fori_loop(1, n_seq, send_cot, 0)

    def send(offset, carry):
        to_seq = lax.rem(seq + offset // n_dp, n_seq)
        to_dp = lax.rem(dp + lax.rem(offset, n_dp), n_dp)
        pltpu.make_async_remote_copy(
            packed.at[:, to_dp, :, to_seq],
            out.at[pl.ds(0, 3), :, me],
            send_sem,
            recv_sem,
            device_id=(to_seq, to_dp),
            device_id_type=MESH,
        ).start()
        return carry

    lax.fori_loop(1, total, send, 0)
    pltpu.make_async_copy(packed.at[:, dp, :, seq], out.at[pl.ds(0, 3), :, me], recv_sem).start()
    pltpu.make_async_copy(
        cot.at[:, :, seq], out.at[3, :, pl.ds(seq * n_dp, n_dp)], cot_recv
    ).start()
    gone = out.at[pl.ds(0, 3), :, pl.ds(0, total - 1)]
    pltpu.make_async_copy(gone, gone, send_sem).wait()
    gone = out.at[3, :, pl.ds(0, total - n_dp)]
    pltpu.make_async_copy(gone, gone, cot_send).wait()
    here = out.at[pl.ds(0, 3)]
    pltpu.make_async_copy(here, here, recv_sem).wait()
    here = out.at[3]
    pltpu.make_async_copy(here, here, cot_recv).wait()


def gather_kernel(n_seq, n_dp, done, grads, att, send_sem, recv_sem, att_send, att_recv):
    seq, dp = lax.axis_index("seq"), lax.axis_index("dp")
    total = n_seq * n_dp
    me = seq * n_dp + dp
    greet_all(seq, dp, n_seq, n_dp)

    def send_att(offset, carry):
        peer = lax.rem(seq + offset, n_seq)
        pltpu.make_async_remote_copy(
            done.at[0, :, pl.ds(peer * n_dp, n_dp)],
            att.at[:, :, seq],
            att_send,
            att_recv,
            device_id=(peer, dp),
            device_id_type=MESH,
        ).start()
        return carry

    lax.fori_loop(1, n_seq, send_att, 0)

    def send(offset, carry):
        to_seq = lax.rem(seq + offset // n_dp, n_seq)
        to_dp = lax.rem(dp + lax.rem(offset, n_dp), n_dp)
        pltpu.make_async_remote_copy(
            done.at[pl.ds(1, 3), :, to_seq * n_dp + to_dp],
            grads.at[:, dp, :, seq],
            send_sem,
            recv_sem,
            device_id=(to_seq, to_dp),
            device_id_type=MESH,
        ).start()
        return carry

    lax.fori_loop(1, total, send, 0)
    pltpu.make_async_copy(done.at[pl.ds(1, 3), :, me], grads.at[:, dp, :, seq], recv_sem).start()
    pltpu.make_async_copy(
        done.at[0, :, pl.ds(seq * n_dp, n_dp)], att.at[:, :, seq], att_recv
    ).start()
    gone = done.at[pl.ds(0, 3), :, pl.ds(0, total - 1)]
    pltpu.make_async_copy(gone, gone, send_sem).wait()
    gone = done.at[0, :, pl.ds(0, total - n_dp)]
    pltpu.make_async_copy(gone, gone, att_send).wait()
    pltpu.make_async_copy(grads, grads, recv_sem).wait()
    pltpu.make_async_copy(att, att, att_recv).wait()


def scatter(packed, cot, n_seq, n_dp):
    cap = packed.shape[2]
    return pl.pallas_call(
        functools.partial(scatter_kernel, n_seq, n_dp),
        out_shape=jax.ShapeDtypeStruct((4, cap, n_seq * n_dp) + packed.shape[4:], packed.dtype),
        in_specs=[pl.BlockSpec(memory_space=pltpu.VMEM)] * 2,
        out_specs=pl.BlockSpec(memory_space=pltpu.VMEM),
        scratch_shapes=[pltpu.SemaphoreType.DMA] * 4,
        compiler_params=pltpu.CompilerParams(
            collective_id=0, has_side_effects=True, vmem_limit_bytes=40 << 20
        ),
        name="scatter_to_heads",
    )(packed, cot)


def gather(done, n_seq, n_dp):
    cap, tail = done.shape[1], done.shape[3:]
    return pl.pallas_call(
        functools.partial(gather_kernel, n_seq, n_dp),
        out_shape=(
            jax.ShapeDtypeStruct((3, n_dp, cap, n_seq) + tail, done.dtype),
            jax.ShapeDtypeStruct((cap, n_dp, n_seq) + tail, done.dtype),
        ),
        in_specs=[pl.BlockSpec(memory_space=pltpu.VMEM)],
        out_specs=(pl.BlockSpec(memory_space=pltpu.VMEM),) * 2,
        scratch_shapes=[pltpu.SemaphoreType.DMA] * 4,
        compiler_params=pltpu.CompilerParams(
            collective_id=1, has_side_effects=True, vmem_limit_bytes=40 << 20
        ),
        name="gather_from_heads",
    )(done)


def dot(a, b, dim_a, dim_b):
    return lax.dot_general(
        a, b, (((dim_a,), (dim_b,)), ((), ())), preferred_element_type=jnp.float32
    )


def attention_kernel(blocks, first_ref, live_ref, data, start, out, dk_acc, dv_acc):
    size = BLOCK
    scale = HEAD ** (-0.5)
    dk_acc[...] = jnp.zeros_like(dk_acc)
    dv_acc[...] = jnp.zeros_like(dv_acc)
    key_iota = lax.broadcasted_iota(jnp.int32, (size, size), 0)
    query_iota = lax.broadcasted_iota(jnp.int32, (size, size), 1)

    def query_block(i, carry):
        rows = pl.ds(pl.multiple_of(i * size, size), size)
        q = data[0, 0, rows, :]
        do = data[3, 0, rows, :]
        low = start[i]
        first = first_ref[i]

        def tile(j):
            keys = pl.ds(pl.multiple_of(j * size, size), size)
            k = data[1, 0, keys, :]
            v = data[2, 0, keys, :]
            scores = dot(k, q, 1, 1) * (scale * LOG2E)
            allowed = (key_iota >= low - j * size) & (key_iota <= query_iota + (i - j) * size)
            return keys, k, v, scores, allowed

        def forward(j, state):
            top, total, acc = state
            keys, k, v, scores, allowed = tile(j)
            scores = jnp.where(allowed, scores, NEGATIVE_FILL)
            new_top = jnp.maximum(top, jnp.max(scores, axis=0, keepdims=True))
            weight = jnp.where(allowed, jnp.exp2(scores - new_top), 0.0)
            shrink = jnp.exp2(top - new_top)
            total = total * shrink + jnp.sum(weight, axis=0, keepdims=True)
            acc = acc * shrink + dot(v, weight.astype(jnp.bfloat16), 0, 0)
            return new_top, total, acc

        top, total, acc = lax.fori_loop(
            first,
            i + 1,
            forward,
            (
                jnp.full((1, size), NEGATIVE_FILL, jnp.float32),
                jnp.zeros((1, size), jnp.float32),
                jnp.zeros((HEAD, size), jnp.float32),
            ),
        )
        log_total = top + jnp.log2(total)
        attended = jnp.transpose(acc / total).astype(jnp.bfloat16)
        row_ids = i * size + lax.broadcasted_iota(jnp.int32, (size, HEAD), 0)
        attended = jnp.where(row_ids < live_ref[0], attended, jnp.zeros_like(attended))
        out[0, 0, rows, :] = attended
        delta = jnp.sum(
            jnp.transpose(do.astype(jnp.float32) * attended.astype(jnp.float32)),
            axis=0,
            keepdims=True,
        )

        def backward(j, grad_q):
            keys, k, v, scores, allowed = tile(j)
            weight = jnp.where(allowed, jnp.exp2(scores - log_total), 0.0)
            grad_prob = dot(v, do, 1, 1)
            grad_score = (weight * (grad_prob - delta)).astype(jnp.bfloat16)
            dv_acc[keys, :] += dot(weight.astype(jnp.bfloat16), do, 1, 0)
            dk_acc[keys, :] += dot(grad_score, q, 1, 0)
            return grad_q + dot(k, grad_score, 0, 0)

        grad_q = lax.fori_loop(
            first, i + 1, backward, jnp.zeros((HEAD, size), jnp.float32)
        )
        out[1, 0, rows, :] = jnp.transpose(grad_q * scale).astype(jnp.bfloat16)
        return carry

    lax.fori_loop(0, blocks, query_block, 0)

    def finish(i, carry):
        rows = pl.ds(pl.multiple_of(i * size, size), size)
        out[2, 0, rows, :] = (dk_acc[rows, :] * scale).astype(jnp.bfloat16)
        out[3, 0, rows, :] = dv_acc[rows, :].astype(jnp.bfloat16)
        return carry

    lax.fori_loop(0, blocks, finish, 0)


def attend(data, start, live):
    _, heads, rows, width = data.shape
    blocks = rows // BLOCK
    spec = pl.BlockSpec((4, 1, rows, width), lambda h, *_: (0, h, 0, 0))
    return pl.pallas_call(
        functools.partial(attention_kernel, blocks),
        out_shape=jax.ShapeDtypeStruct(data.shape, data.dtype),
        grid_spec=pltpu.PrefetchScalarGridSpec(
            num_scalar_prefetch=2,
            grid=(heads,),
            in_specs=[spec, pl.BlockSpec((blocks, 1, BLOCK), lambda h, *_: (0, 0, 0))],
            out_specs=spec,
            scratch_shapes=[pltpu.VMEM((rows, width), jnp.float32)] * 2,
        ),
        compiler_params=pltpu.CompilerParams(
            dimension_semantics=("arbitrary",), vmem_limit_bytes=60 << 20
        ),
        name="attend_group",
    )(start[::BLOCK] // BLOCK, live, data, start.reshape(blocks, 1, BLOCK))


def body(queries, keys_in, values, grad_out, doc_lengths, doc_group):
    n_seq = lax.axis_size("seq")
    n_dp = lax.axis_size("dp")
    devices = n_seq * n_dp
    local_rows = queries.shape[0]
    features = queries.shape[2]
    local_heads = features // (n_seq * HEAD)
    cap = grad_out.shape[0]
    tail = (n_seq, local_heads, HEAD)
    doc_ends, group_units, first_unit = group_tables(doc_lengths, doc_group, n_dp, devices)
    slots = jnp.arange(cap, dtype=jnp.int32)[None, :]
    source_row = jnp.minimum(first_unit[:, None] + slots, local_rows - 1).reshape(-1)
    row_ids = jnp.arange(local_rows, dtype=jnp.int32)
    row_group = jnp.sum((first_unit + group_units)[None, :] <= row_ids[:, None], axis=1)
    target_row = row_group * cap + row_ids - jnp.take(first_unit, row_group)

    packed = jnp.stack(
        [
            jnp.take(part.reshape(local_rows, features), source_row, axis=0)
            for part in (queries, keys_in, values)
        ]
    )
    arrived = scatter(
        packed.reshape((3, n_dp, cap) + tail), grad_out.reshape((cap, n_dp) + tail), n_seq, n_dp
    )
    rows = cap * devices
    data = jnp.transpose(arrived.reshape(4, rows, local_heads, HEAD), (0, 2, 1, 3))

    group = lax.axis_index("dp")
    base = first_unit[group] * devices
    live = group_units[group] * devices
    local_ids = jnp.arange(rows, dtype=jnp.int32)
    doc_starts = doc_ends - doc_lengths
    begun = doc_starts[None, :] <= (base + local_ids)[:, None]
    start = jnp.max(jnp.where(begun, doc_starts[None, :] - base, 0), axis=1)
    start = jnp.where(local_ids < live, start, local_ids).astype(jnp.int32)
    done = attend(data, start, live.astype(jnp.int32).reshape(1))

    done = jnp.transpose(done, (0, 2, 1, 3)).reshape(4, cap, devices, local_heads, HEAD)
    grads, attended = gather(done, n_seq, n_dp)
    grads = grads.reshape(3, n_dp * cap, features)
    outs = [
        jnp.take(grads[part], target_row, axis=0).reshape(local_rows, 1, features)
        for part in range(3)
    ]
    return (attended.reshape(cap, n_dp, features),) + tuple(outs)


def solution(mesh):
    return jax.shard_map(
        body,
        mesh=mesh,
        in_specs=(
            P(None, ("seq", "dp"), None),
            P(None, ("seq", "dp"), None),
            P(None, ("seq", "dp"), None),
            P(None, ("seq", "dp"), None),
            P(),
            P(),
        ),
        out_specs=(
            P(None, ("seq", "dp"), None),
            P(None, ("seq", "dp"), None),
            P(None, ("seq", "dp"), None),
            P(None, ("seq", "dp"), None),
        ),
        check_vma=False,
    )
```

```python
import functools

import jax
import jax.numpy as jnp
import numpy as np
from jax import lax
from jax.experimental import pallas as pl
from jax.experimental.pallas import tpu as pltpu
from jax.sharding import PartitionSpec as P

HEAD = 128
NEGATIVE_FILL = -1e30
LOG2E = 1.4426950408889634
BLOCK = 512
MESH = pl.DeviceIdType.MESH


def group_tables(doc_lengths, doc_group, group_count, per_unit):
    doc_ends = jnp.cumsum(doc_lengths)
    member = (doc_group[:, None] == jnp.arange(group_count, dtype=jnp.int32)[None, :]).astype(
        jnp.int32
    )
    group_units = jnp.sum(member * doc_lengths[:, None], axis=0) // per_unit
    first_unit = jnp.cumsum(group_units) - group_units
    return (doc_ends, group_units, first_unit)


def greet_all(seq, dp, n_seq, n_dp):
    me = seq * n_dp + dp
    total = n_seq * n_dp
    barrier = pltpu.get_barrier_semaphore()

    def greet(offset, carry):
        peer = lax.rem(me + offset, total)
        pl.semaphore_signal(
            barrier, 1, device_id=(peer // n_dp, lax.rem(peer, n_dp)), device_id_type=MESH
        )
        return carry

    lax.fori_loop(1, total, greet, 0)
    pl.semaphore_wait(barrier, total - 1)


def scatter_kernel(n_seq, n_dp, packed, cot, out, send_sem, recv_sem, cot_send, cot_recv):
    seq, dp = lax.axis_index("seq"), lax.axis_index("dp")
    total = n_seq * n_dp
    me = seq * n_dp + dp
    greet_all(seq, dp, n_seq, n_dp)

    def send_cot(offset, carry):
        peer = lax.rem(seq + offset, n_seq)
        pltpu.make_async_remote_copy(
            cot.at[:, :, peer],
            out.at[3, :, pl.ds(seq * n_dp, n_dp)],
            cot_send,
            cot_recv,
            device_id=(peer, dp),
            device_id_type=MESH,
        ).start()
        return carry

    lax.fori_loop(1, n_seq, send_cot, 0)

    def send(offset, carry):
        to_seq = lax.rem(seq + offset // n_dp, n_seq)
        to_dp = lax.rem(dp + lax.rem(offset, n_dp), n_dp)
        pltpu.make_async_remote_copy(
            packed.at[:, to_dp, :, to_seq],
            out.at[pl.ds(0, 3), :, me],
            send_sem,
            recv_sem,
            device_id=(to_seq, to_dp),
            device_id_type=MESH,
        ).start()
        return carry

    lax.fori_loop(1, total, send, 0)
    pltpu.make_async_copy(packed.at[:, dp, :, seq], out.at[pl.ds(0, 3), :, me], recv_sem).start()
    pltpu.make_async_copy(
        cot.at[:, :, seq], out.at[3, :, pl.ds(seq * n_dp, n_dp)], cot_recv
    ).start()
    gone = out.at[pl.ds(0, 3), :, pl.ds(0, total - 1)]
    pltpu.make_async_copy(gone, gone, send_sem).wait()
    gone = out.at[3, :, pl.ds(0, total - n_dp)]
    pltpu.make_async_copy(gone, gone, cot_send).wait()
    here = out.at[pl.ds(0, 3)]
    pltpu.make_async_copy(here, here, recv_sem).wait()
    here = out.at[3]
    pltpu.make_async_copy(here, here, cot_recv).wait()


def gather_kernel(n_seq, n_dp, done, grads, att, send_sem, recv_sem, att_send, att_recv):
    seq, dp = lax.axis_index("seq"), lax.axis_index("dp")
    total = n_seq * n_dp
    me = seq * n_dp + dp
    greet_all(seq, dp, n_seq, n_dp)

    def send_att(offset, carry):
        peer = lax.rem(seq + offset, n_seq)
        pltpu.make_async_remote_copy(
            done.at[0, :, pl.ds(peer * n_dp, n_dp)],
            att.at[:, :, seq],
            att_send,
            att_recv,
            device_id=(peer, dp),
            device_id_type=MESH,
        ).start()
        return carry

    lax.fori_loop(1, n_seq, send_att, 0)

    def send(offset, carry):
        to_seq = lax.rem(seq + offset // n_dp, n_seq)
        to_dp = lax.rem(dp + lax.rem(offset, n_dp), n_dp)
        pltpu.make_async_remote_copy(
            done.at[pl.ds(1, 3), :, to_seq * n_dp + to_dp],
            grads.at[:, dp, :, seq],
            send_sem,
            recv_sem,
            device_id=(to_seq, to_dp),
            device_id_type=MESH,
        ).start()
        return carry

    lax.fori_loop(1, total, send, 0)
    pltpu.make_async_copy(done.at[pl.ds(1, 3), :, me], grads.at[:, dp, :, seq], recv_sem).start()
    pltpu.make_async_copy(
        done.at[0, :, pl.ds(seq * n_dp, n_dp)], att.at[:, :, seq], att_recv
    ).start()
    gone = done.at[pl.ds(0, 3), :, pl.ds(0, total - 1)]
    pltpu.make_async_copy(gone, gone, send_sem).wait()
    gone = done.at[0, :, pl.ds(0, total - n_dp)]
    pltpu.make_async_copy(gone, gone, att_send).wait()
    pltpu.make_async_copy(grads, grads, recv_sem).wait()
    pltpu.make_async_copy(att, att, att_recv).wait()


def scatter(packed, cot, n_seq, n_dp):
    cap = packed.shape[2]
    return pl.pallas_call(
        functools.partial(scatter_kernel, n_seq, n_dp),
        out_shape=jax.ShapeDtypeStruct((4, cap, n_seq * n_dp) + packed.shape[4:], packed.dtype),
        in_specs=[pl.BlockSpec(memory_space=pltpu.VMEM)] * 2,
        out_specs=pl.BlockSpec(memory_space=pltpu.VMEM),
        scratch_shapes=[pltpu.SemaphoreType.DMA] * 4,
        compiler_params=pltpu.CompilerParams(
            collective_id=0, has_side_effects=True, vmem_limit_bytes=40 << 20
        ),
        name="scatter_to_heads",
    )(packed, cot)


def gather(done, n_seq, n_dp):
    cap, tail = done.shape[1], done.shape[3:]
    return pl.pallas_call(
        functools.partial(gather_kernel, n_seq, n_dp),
        out_shape=(
            jax.ShapeDtypeStruct((3, n_dp, cap, n_seq) + tail, done.dtype),
            jax.ShapeDtypeStruct((cap, n_dp, n_seq) + tail, done.dtype),
        ),
        in_specs=[pl.BlockSpec(memory_space=pltpu.VMEM)],
        out_specs=(pl.BlockSpec(memory_space=pltpu.VMEM),) * 2,
        scratch_shapes=[pltpu.SemaphoreType.DMA] * 4,
        compiler_params=pltpu.CompilerParams(
            collective_id=1, has_side_effects=True, vmem_limit_bytes=40 << 20
        ),
        name="gather_from_heads",
    )(done)


def dot(a, b, dim_a, dim_b):
    return lax.dot_general(
        a, b, (((dim_a,), (dim_b,)), ((), ())), preferred_element_type=jnp.float32
    )


def attention_kernel(blocks, first_ref, live_ref, data, start, out, dk_acc, dv_acc):
    size = BLOCK
    scale = HEAD ** (-0.5)
    dk_acc[...] = jnp.zeros_like(dk_acc)
    dv_acc[...] = jnp.zeros_like(dv_acc)
    key_iota = lax.broadcasted_iota(jnp.int32, (size, size), 0)
    query_iota = lax.broadcasted_iota(jnp.int32, (size, size), 1)

    def query_block(i, carry):
        rows = pl.ds(pl.multiple_of(i * size, size), size)
        q = data[0, 0, rows, :]
        do = data[3, 0, rows, :]
        low = start[i]
        first = first_ref[i]

        def tile(j, diagonal):
            keys = pl.ds(pl.multiple_of(j * size, size), size)
            k = data[1, 0, keys, :]
            v = data[2, 0, keys, :]
            scores = dot(k, q, 1, 1) * (scale * LOG2E)
            allowed = key_iota >= low - j * size
            if diagonal:
                allowed = allowed & (key_iota <= query_iota)
            return keys, k, v, jnp.where(allowed, scores, NEGATIVE_FILL)

        def forward(j, state, diagonal=False):
            top, total, acc = state
            keys, k, v, scores = tile(j, diagonal)
            new_top = jnp.maximum(top, jnp.max(scores, axis=0, keepdims=True))
            weight = jnp.exp2(scores - new_top)
            shrink = jnp.exp2(top - new_top)
            total = total * shrink + jnp.sum(weight, axis=0, keepdims=True)
            acc = acc * shrink + dot(v, weight.astype(jnp.bfloat16), 0, 0)
            return new_top, total, acc

        state = lax.fori_loop(
            first,
            i,
            forward,
            (
                jnp.full((1, size), NEGATIVE_FILL, jnp.float32),
                jnp.zeros((1, size), jnp.float32),
                jnp.zeros((HEAD, size), jnp.float32),
            ),
        )
        top, total, acc = forward(i, state, True)
        log_total = top + jnp.log2(total)
        attended = jnp.transpose(acc / total).astype(jnp.bfloat16)
        row_ids = i * size + lax.broadcasted_iota(jnp.int32, (size, HEAD), 0)
        attended = jnp.where(row_ids < live_ref[0], attended, jnp.zeros_like(attended))
        out[0, 0, rows, :] = attended
        delta = jnp.sum(
            jnp.transpose(do.astype(jnp.float32) * attended.astype(jnp.float32)),
            axis=0,
            keepdims=True,
        )

        def backward(j, grad_q, diagonal=False):
            keys, k, v, scores = tile(j, diagonal)
            weight = jnp.exp2(scores - log_total)
            grad_prob = dot(v, do, 1, 1)
            grad_score = (weight * (grad_prob - delta)).astype(jnp.bfloat16)
            dv_acc[keys, :] += dot(weight.astype(jnp.bfloat16), do, 1, 0)
            dk_acc[keys, :] += dot(grad_score, q, 1, 0)
            return grad_q + dot(k, grad_score, 0, 0)

        grad_q = lax.fori_loop(first, i, backward, jnp.zeros((HEAD, size), jnp.float32))
        grad_q = backward(i, grad_q, True)
        out[1, 0, rows, :] = jnp.transpose(grad_q * scale).astype(jnp.bfloat16)
        return carry

    lax.fori_loop(0, blocks, query_block, 0)

    def finish(i, carry):
        rows = pl.ds(pl.multiple_of(i * size, size), size)
        out[2, 0, rows, :] = (dk_acc[rows, :] * scale).astype(jnp.bfloat16)
        out[3, 0, rows, :] = dv_acc[rows, :].astype(jnp.bfloat16)
        return carry

    lax.fori_loop(0, blocks, finish, 0)


def attend(data, start, live):
    _, heads, rows, width = data.shape
    blocks = rows // BLOCK
    spec = pl.BlockSpec((4, 1, rows, width), lambda h, *_: (0, h, 0, 0))
    return pl.pallas_call(
        functools.partial(attention_kernel, blocks),
        out_shape=jax.ShapeDtypeStruct(data.shape, data.dtype),
        grid_spec=pltpu.PrefetchScalarGridSpec(
            num_scalar_prefetch=2,
            grid=(heads,),
            in_specs=[spec, pl.BlockSpec((blocks, 1, BLOCK), lambda h, *_: (0, 0, 0))],
            out_specs=spec,
            scratch_shapes=[pltpu.VMEM((rows, width), jnp.float32)] * 2,
        ),
        compiler_params=pltpu.CompilerParams(
            dimension_semantics=("arbitrary",), vmem_limit_bytes=60 << 20
        ),
        name="attend_group",
    )(start[::BLOCK] // BLOCK, live, data, start.reshape(blocks, 1, BLOCK))


def body(queries, keys_in, values, grad_out, doc_lengths, doc_group):
    n_seq = lax.axis_size("seq")
    n_dp = lax.axis_size("dp")
    devices = n_seq * n_dp
    local_rows = queries.shape[0]
    features = queries.shape[2]
    local_heads = features // (n_seq * HEAD)
    cap = grad_out.shape[0]
    tail = (n_seq, local_heads, HEAD)
    doc_ends, group_units, first_unit = group_tables(doc_lengths, doc_group, n_dp, devices)
    slots = jnp.arange(cap, dtype=jnp.int32)[None, :]
    source_row = jnp.minimum(first_unit[:, None] + slots, local_rows - 1).reshape(-1)
    row_ids = jnp.arange(local_rows, dtype=jnp.int32)
    row_group = jnp.sum((first_unit + group_units)[None, :] <= row_ids[:, None], axis=1)
    target_row = row_group * cap + row_ids - jnp.take(first_unit, row_group)

    whole = jnp.concatenate(
        [part.reshape(local_rows, features) for part in (queries, keys_in, values)], axis=0
    )
    part_base = jnp.arange(3, dtype=jnp.int32)[:, None]
    packed = jnp.take(
        whole, (source_row[None, :] + part_base * local_rows).reshape(-1), axis=0, mode="clip"
    )
    arrived = scatter(
        packed.reshape((3, n_dp, cap) + tail), grad_out.reshape((cap, n_dp) + tail), n_seq, n_dp
    )
    rows = cap * devices
    data = jnp.transpose(arrived.reshape(4, rows, local_heads, HEAD), (0, 2, 1, 3))

    group = lax.axis_index("dp")
    base = first_unit[group] * devices
    live = group_units[group] * devices
    local_ids = jnp.arange(rows, dtype=jnp.int32)
    doc_starts = doc_ends - doc_lengths
    begun = doc_starts[None, :] <= (base + local_ids)[:, None]
    start = jnp.max(jnp.where(begun, doc_starts[None, :] - base, 0), axis=1)
    start = jnp.where(local_ids < live, start, local_ids).astype(jnp.int32)
    done = attend(data, start, live.astype(jnp.int32).reshape(1))

    done = jnp.transpose(done, (0, 2, 1, 3)).reshape(4, cap, devices, local_heads, HEAD)
    grads, attended = gather(done, n_seq, n_dp)
    grads = grads.reshape(3 * n_dp * cap, features)
    outs = [
        jnp.take(grads, target_row + part * n_dp * cap, axis=0, mode="clip").reshape(
            local_rows, 1, features
        )
        for part in range(3)
    ]
    return (attended.reshape(cap, n_dp, features),) + tuple(outs)


def solution(mesh):
    return jax.shard_map(
        body,
        mesh=mesh,
        in_specs=(
            P(None, ("seq", "dp"), None),
            P(None, ("seq", "dp"), None),
            P(None, ("seq", "dp"), None),
            P(None, ("seq", "dp"), None),
            P(),
            P(),
        ),
        out_specs=(
            P(None, ("seq", "dp"), None),
            P(None, ("seq", "dp"), None),
            P(None, ("seq", "dp"), None),
            P(None, ("seq", "dp"), None),
        ),
        check_vma=False,
    )
```

```python
import functools

import jax
import jax.numpy as jnp
import numpy as np
from jax import lax
from jax.experimental import pallas as pl
from jax.experimental.pallas import tpu as pltpu
from jax.sharding import PartitionSpec as P

HEAD = 128
NEGATIVE_FILL = -1e30
LOG2E = 1.4426950408889634
BLOCK = 512
MESH = pl.DeviceIdType.MESH


def group_tables(doc_lengths, doc_group, group_count, per_unit):
    doc_ends = jnp.cumsum(doc_lengths)
    member = (doc_group[:, None] == jnp.arange(group_count, dtype=jnp.int32)[None, :]).astype(
        jnp.int32
    )
    group_units = jnp.sum(member * doc_lengths[:, None], axis=0) // per_unit
    first_unit = jnp.cumsum(group_units) - group_units
    return (doc_ends, group_units, first_unit)


def greet_all(seq, dp, n_seq, n_dp):
    me = seq * n_dp + dp
    total = n_seq * n_dp
    barrier = pltpu.get_barrier_semaphore()

    def greet(offset, carry):
        peer = lax.rem(me + offset, total)
        pl.semaphore_signal(
            barrier, 1, device_id=(peer // n_dp, lax.rem(peer, n_dp)), device_id_type=MESH
        )
        return carry

    lax.fori_loop(1, total, greet, 0)
    pl.semaphore_wait(barrier, total - 1)


def scatter_kernel(n_seq, n_dp, packed, cot, out, send_sem, recv_sem, cot_send, cot_recv):
    seq, dp = lax.axis_index("seq"), lax.axis_index("dp")
    total = n_seq * n_dp
    me = seq * n_dp + dp
    greet_all(seq, dp, n_seq, n_dp)

    def send_cot(offset, carry):
        peer = lax.rem(seq + offset, n_seq)
        pltpu.make_async_remote_copy(
            cot.at[:, :, peer],
            out.at[3, :, pl.ds(seq * n_dp, n_dp)],
            cot_send,
            cot_recv,
            device_id=(peer, dp),
            device_id_type=MESH,
        ).start()
        return carry

    lax.fori_loop(1, n_seq, send_cot, 0)

    def send(offset, carry):
        to_seq = lax.rem(seq + offset // n_dp, n_seq)
        to_dp = lax.rem(dp + lax.rem(offset, n_dp), n_dp)
        pltpu.make_async_remote_copy(
            packed.at[:, to_dp, :, to_seq],
            out.at[pl.ds(0, 3), :, me],
            send_sem,
            recv_sem,
            device_id=(to_seq, to_dp),
            device_id_type=MESH,
        ).start()
        return carry

    lax.fori_loop(1, total, send, 0)
    pltpu.make_async_copy(packed.at[:, dp, :, seq], out.at[pl.ds(0, 3), :, me], recv_sem).start()
    pltpu.make_async_copy(
        cot.at[:, :, seq], out.at[3, :, pl.ds(seq * n_dp, n_dp)], cot_recv
    ).start()
    gone = out.at[pl.ds(0, 3), :, pl.ds(0, total - 1)]
    pltpu.make_async_copy(gone, gone, send_sem).wait()
    gone = out.at[3, :, pl.ds(0, total - n_dp)]
    pltpu.make_async_copy(gone, gone, cot_send).wait()
    here = out.at[pl.ds(0, 3)]
    pltpu.make_async_copy(here, here, recv_sem).wait()
    here = out.at[3]
    pltpu.make_async_copy(here, here, cot_recv).wait()


def gather_kernel(n_seq, n_dp, done, grads, att, send_sem, recv_sem, att_send, att_recv):
    seq, dp = lax.axis_index("seq"), lax.axis_index("dp")
    total = n_seq * n_dp
    me = seq * n_dp + dp
    greet_all(seq, dp, n_seq, n_dp)

    def send_att(offset, carry):
        peer = lax.rem(seq + offset, n_seq)
        pltpu.make_async_remote_copy(
            done.at[0, :, pl.ds(peer * n_dp, n_dp)],
            att.at[:, :, seq],
            att_send,
            att_recv,
            device_id=(peer, dp),
            device_id_type=MESH,
        ).start()
        return carry

    lax.fori_loop(1, n_seq, send_att, 0)

    def send(offset, carry):
        to_seq = lax.rem(seq + offset // n_dp, n_seq)
        to_dp = lax.rem(dp + lax.rem(offset, n_dp), n_dp)
        pltpu.make_async_remote_copy(
            done.at[pl.ds(1, 3), :, to_seq * n_dp + to_dp],
            grads.at[:, dp, :, seq],
            send_sem,
            recv_sem,
            device_id=(to_seq, to_dp),
            device_id_type=MESH,
        ).start()
        return carry

    lax.fori_loop(1, total, send, 0)
    pltpu.make_async_copy(done.at[pl.ds(1, 3), :, me], grads.at[:, dp, :, seq], recv_sem).start()
    pltpu.make_async_copy(
        done.at[0, :, pl.ds(seq * n_dp, n_dp)], att.at[:, :, seq], att_recv
    ).start()
    gone = done.at[pl.ds(0, 3), :, pl.ds(0, total - 1)]
    pltpu.make_async_copy(gone, gone, send_sem).wait()
    gone = done.at[0, :, pl.ds(0, total - n_dp)]
    pltpu.make_async_copy(gone, gone, att_send).wait()
    pltpu.make_async_copy(grads, grads, recv_sem).wait()
    pltpu.make_async_copy(att, att, att_recv).wait()


def scatter(packed, cot, n_seq, n_dp):
    cap = packed.shape[2]
    return pl.pallas_call(
        functools.partial(scatter_kernel, n_seq, n_dp),
        out_shape=jax.ShapeDtypeStruct((4, cap, n_seq * n_dp) + packed.shape[4:], packed.dtype),
        in_specs=[pl.BlockSpec(memory_space=pltpu.VMEM)] * 2,
        out_specs=pl.BlockSpec(memory_space=pltpu.VMEM),
        scratch_shapes=[pltpu.SemaphoreType.DMA] * 4,
        compiler_params=pltpu.CompilerParams(
            collective_id=0, has_side_effects=True, vmem_limit_bytes=24 << 20
        ),
        name="scatter_to_heads",
    )(packed, cot)


def gather(done, n_seq, n_dp):
    cap, tail = done.shape[1], done.shape[3:]
    return pl.pallas_call(
        functools.partial(gather_kernel, n_seq, n_dp),
        out_shape=(
            jax.ShapeDtypeStruct((3, n_dp, cap, n_seq) + tail, done.dtype),
            jax.ShapeDtypeStruct((cap, n_dp, n_seq) + tail, done.dtype),
        ),
        in_specs=[pl.BlockSpec(memory_space=pltpu.VMEM)],
        out_specs=(pl.BlockSpec(memory_space=pltpu.VMEM),) * 2,
        scratch_shapes=[pltpu.SemaphoreType.DMA] * 4,
        compiler_params=pltpu.CompilerParams(
            collective_id=1, has_side_effects=True, vmem_limit_bytes=24 << 20
        ),
        name="gather_from_heads",
    )(done)


def dot(a, b, dim_a, dim_b):
    return lax.dot_general(
        a, b, (((dim_a,), (dim_b,)), ((), ())), preferred_element_type=jnp.float32
    )


def attention_kernel(blocks, first_ref, live_ref, data, start, out, dk_acc, dv_acc):
    size = BLOCK
    scale = HEAD ** (-0.5)
    dk_acc[...] = jnp.zeros_like(dk_acc)
    dv_acc[...] = jnp.zeros_like(dv_acc)
    key_iota = lax.broadcasted_iota(jnp.int32, (size, size), 0)
    query_iota = lax.broadcasted_iota(jnp.int32, (size, size), 1)

    def query_block(i, carry):
        rows = pl.ds(pl.multiple_of(i * size, size), size)
        q = data[0, 0, rows, :]
        do = data[3, 0, rows, :]
        low = start[i]
        first = first_ref[i]

        def tile(j, diagonal):
            keys = pl.ds(pl.multiple_of(j * size, size), size)
            k = data[1, 0, keys, :]
            v = data[2, 0, keys, :]
            scores = dot(k, q, 1, 1) * (scale * LOG2E)
            allowed = key_iota >= low - j * size
            if diagonal:
                allowed = allowed & (key_iota <= query_iota)
            return keys, k, v, jnp.where(allowed, scores, NEGATIVE_FILL)

        def forward(j, state, diagonal=False):
            top, total, acc = state
            keys, k, v, scores = tile(j, diagonal)
            new_top = jnp.maximum(top, jnp.max(scores, axis=0, keepdims=True))
            weight = jnp.exp2(scores - new_top)
            shrink = jnp.exp2(top - new_top)
            total = total * shrink + jnp.sum(weight, axis=0, keepdims=True)
            acc = acc * shrink + dot(v, weight.astype(jnp.bfloat16), 0, 0)
            return new_top, total, acc

        state = lax.fori_loop(
            first,
            i,
            forward,
            (
                jnp.full((1, size), NEGATIVE_FILL, jnp.float32),
                jnp.zeros((1, size), jnp.float32),
                jnp.zeros((HEAD, size), jnp.float32),
            ),
        )
        top, total, acc = forward(i, state, True)
        log_total = top + jnp.log2(total)
        attended = jnp.transpose(acc / total).astype(jnp.bfloat16)
        row_ids = i * size + lax.broadcasted_iota(jnp.int32, (size, HEAD), 0)
        attended = jnp.where(row_ids < live_ref[0], attended, jnp.zeros_like(attended))
        out[0, 0, rows, :] = attended
        delta = jnp.sum(
            jnp.transpose(do.astype(jnp.float32) * attended.astype(jnp.float32)),
            axis=0,
            keepdims=True,
        )

        def backward(j, grad_q, diagonal=False):
            keys, k, v, scores = tile(j, diagonal)
            weight = jnp.exp2(scores - log_total)
            grad_prob = dot(v, do, 1, 1)
            grad_score = (weight * (grad_prob - delta)).astype(jnp.bfloat16)
            dv_acc[keys, :] += dot(weight.astype(jnp.bfloat16), do, 1, 0)
            dk_acc[keys, :] += dot(grad_score, q, 1, 0)
            return grad_q + dot(k, grad_score, 0, 0)

        grad_q = lax.fori_loop(first, i, backward, jnp.zeros((HEAD, size), jnp.float32))
        grad_q = backward(i, grad_q, True)
        out[1, 0, rows, :] = jnp.transpose(grad_q * scale).astype(jnp.bfloat16)
        return carry

    lax.fori_loop(0, blocks, query_block, 0)

    def finish(i, carry):
        rows = pl.ds(pl.multiple_of(i * size, size), size)
        out[2, 0, rows, :] = (dk_acc[rows, :] * scale).astype(jnp.bfloat16)
        out[3, 0, rows, :] = dv_acc[rows, :].astype(jnp.bfloat16)
        return carry

    lax.fori_loop(0, blocks, finish, 0)


def attend(data, start, live):
    _, heads, rows, width = data.shape
    blocks = rows // BLOCK
    spec = pl.BlockSpec((4, 1, rows, width), lambda h, *_: (0, h, 0, 0))
    return pl.pallas_call(
        functools.partial(attention_kernel, blocks),
        out_shape=jax.ShapeDtypeStruct(data.shape, data.dtype),
        grid_spec=pltpu.PrefetchScalarGridSpec(
            num_scalar_prefetch=2,
            grid=(heads,),
            in_specs=[spec, pl.BlockSpec((blocks, 1, BLOCK), lambda h, *_: (0, 0, 0))],
            out_specs=spec,
            scratch_shapes=[pltpu.VMEM((rows, width), jnp.float32)] * 2,
        ),
        compiler_params=pltpu.CompilerParams(
            dimension_semantics=("arbitrary",), vmem_limit_bytes=32 << 20
        ),
        name="attend_group",
    )(start[::BLOCK] // BLOCK, live, data, start.reshape(blocks, 1, BLOCK))


def body(queries, keys_in, values, grad_out, doc_lengths, doc_group):
    n_seq = lax.axis_size("seq")
    n_dp = lax.axis_size("dp")
    devices = n_seq * n_dp
    local_rows = queries.shape[0]
    features = queries.shape[2]
    local_heads = features // (n_seq * HEAD)
    cap = grad_out.shape[0]
    tail = (n_seq, local_heads, HEAD)
    doc_ends, group_units, first_unit = group_tables(doc_lengths, doc_group, n_dp, devices)
    slots = jnp.arange(cap, dtype=jnp.int32)[None, :]
    source_row = jnp.minimum(first_unit[:, None] + slots, local_rows - 1).reshape(-1)
    row_ids = jnp.arange(local_rows, dtype=jnp.int32)
    row_group = jnp.sum((first_unit + group_units)[None, :] <= row_ids[:, None], axis=1)
    group_ids = jnp.arange(n_dp, dtype=jnp.int32)[None, :]
    shift = jnp.where(group_ids == row_group[:, None], group_ids * cap - first_unit[None, :], 0)
    target_row = row_ids + jnp.sum(shift, axis=1)

    whole = jnp.concatenate(
        [part.reshape(local_rows, features) for part in (queries, keys_in, values)], axis=0
    )
    part_base = jnp.arange(3, dtype=jnp.int32)[:, None]
    packed = jnp.take(
        whole, (source_row[None, :] + part_base * local_rows).reshape(-1), axis=0, mode="clip"
    )
    arrived = scatter(
        packed.reshape((3, n_dp, cap) + tail), grad_out.reshape((cap, n_dp) + tail), n_seq, n_dp
    )
    rows = cap * devices
    data = jnp.transpose(arrived.reshape(4, rows, local_heads, HEAD), (0, 2, 1, 3))

    group = lax.axis_index("dp")
    base = first_unit[group] * devices
    live = group_units[group] * devices
    local_ids = jnp.arange(rows, dtype=jnp.int32)
    doc_starts = doc_ends - doc_lengths
    begun = doc_starts[None, :] <= (base + local_ids)[:, None]
    start = jnp.max(jnp.where(begun, doc_starts[None, :] - base, 0), axis=1)
    start = jnp.where(local_ids < live, start, local_ids).astype(jnp.int32)
    done = attend(data, start, live.astype(jnp.int32).reshape(1))

    done = jnp.transpose(done, (0, 2, 1, 3)).reshape(4, cap, devices, local_heads, HEAD)
    grads, attended = gather(done, n_seq, n_dp)
    grads = grads.reshape(3 * n_dp * cap, features)
    outs = [
        jnp.take(grads, target_row + part * n_dp * cap, axis=0, mode="clip").reshape(
            local_rows, 1, features
        )
        for part in range(3)
    ]
    return (attended.reshape(cap, n_dp, features),) + tuple(outs)


def solution(mesh):
    return jax.shard_map(
        body,
        mesh=mesh,
        in_specs=(
            P(None, ("seq", "dp"), None),
            P(None, ("seq", "dp"), None),
            P(None, ("seq", "dp"), None),
            P(None, ("seq", "dp"), None),
            P(),
            P(),
        ),
        out_specs=(
            P(None, ("seq", "dp"), None),
            P(None, ("seq", "dp"), None),
            P(None, ("seq", "dp"), None),
            P(None, ("seq", "dp"), None),
        ),
        check_vma=False,
    )
```
